32 devices in a mesh: grp: 4 (over y, x), seq: 8 (over z, core).
Axes of the slice: x: 2, y: 2, z: 4, core: 2. Of those that a mesh axis runs over, the one named last changes fastest.
Arguments:
- queries: bfloat16 [4096, 1024], P(('grp', 'seq')), may hold values from -6 to 6
- keys: bfloat16 [4096, 1024], P(('grp', 'seq')), may hold values from -11 to 11
- values: bfloat16 [4096, 1024], P(('grp', 'seq')), may hold values from -6 to 6
- forget: float32 [4096, 8], P(('grp', 'seq')), may hold values from 0 to 0.5
- beta: float32 [4096, 8], P(('grp', 'seq')), may hold values from 0 to 1
- level_weights: float32 [9, 4096, 8], P(None, ('grp', 'seq')), may hold values from 0.25 to 2
Outputs:
- output: float32 [4096, 1024], P(('grp', 'seq'))
The draws below stay inside these ranges and needn't reach their ends.
All inputs are finite; a program needn't handle non-finite values.
Results may differ from the reference program's by a relative error of at most 0.0003.
Values sent between devices are 32-bit elements; how exact they have to be, the bound alone decides.
A program may use at most 64 MiB of HBM per device.

```python
import math
import jax
import jax.numpy as jnp
from jax import lax

HEADS = 8
HEAD_DIM = 128
BLOCK = 128
LEVELS = 8
TOK_DEV = 128
TOKENS = 4096
N_GRP = 4
N_SEQ = 8


def slow_heads(key):
    order = jax.random.permutation(jax.random.fold_in(key, 11), HEADS)
    count = HEADS // 2
    return order < count


def device_factor(key, salt):
    factor = jax.random.uniform(jax.random.fold_in(key, salt), (TOKENS // TOK_DEV, HEADS), jnp.float32, 0.6, 1.6)
    return jnp.repeat(factor, TOK_DEV, axis=0)


def draw_keys(key, part):
    subkeys = jax.random.split(jax.random.fold_in(key, 41), 3)
    noise_part = jnp.clip(jax.random.normal(subkeys[0], (TOKENS, HEADS, HEAD_DIM), jnp.float32), -6.0, 6.0)
    sign_pattern = (jax.random.randint(subkeys[1], (HEADS, HEAD_DIM), 0, 2) * 2 - 1).astype(jnp.float32)
    shared_scale = jax.random.uniform(subkeys[2], (TOKENS, HEADS), jnp.float32, 2.4, 3.6)
    result = noise_part + shared_scale[:, :, None] * sign_pattern[None, :, :]
    return result.reshape(TOKENS, HEADS * HEAD_DIM).astype(jnp.bfloat16)


def draw_forget(key, part):
    slow = slow_heads(key)
    subkeys = jax.random.split(jax.random.fold_in(key, 21), 6)
    slow_rate = jax.random.uniform(subkeys[0], (HEADS,), jnp.float32, 0.1, 0.5) / TOKENS
    fast_rate = jax.random.uniform(subkeys[1], (HEADS,), jnp.float32, 1.0 / 500.0, 1.0 / 250.0)
    base_rate = jnp.where(slow, slow_rate, fast_rate)
    rough = jax.random.uniform(subkeys[2], (TOKENS, HEADS), jnp.float32, 0.5, 1.5)
    result = base_rate[None, :] * device_factor(key, 23) * rough
    first_spot = jax.random.randint(subkeys[3], (HEADS,), 0, TOKENS)
    offset = jax.random.randint(subkeys[5], (HEADS,), 1, TOKENS)
    second_spot = (first_spot + offset) % TOKENS
    spots = jnp.stack([first_spot, second_spot], 0)
    amount = jax.random.uniform(subkeys[4], (2, HEADS), jnp.float32, 0.22, 0.4)
    columns = jnp.broadcast_to(jnp.arange(HEADS)[None, :], (2, HEADS))
    return result.at[spots, columns].add(amount)


def draw_beta(key, part):
    slow = slow_heads(key)
    subkeys = jax.random.split(jax.random.fold_in(key, 31), 3)
    slow_base = jax.random.uniform(subkeys[0], (HEADS,), jnp.float32, 0.5, 1.5) * 3.0 * HEAD_DIM / TOKENS
    fast_base = jax.random.uniform(subkeys[1], (HEADS,), jnp.float32, 0.2, 0.7)
    base_value = jnp.where(slow, slow_base, fast_base)
    rough = jax.random.uniform(subkeys[2], (TOKENS, HEADS), jnp.float32, 0.7, 1.3)
    return base_value[None, :] * rough


def block_scale(own_key, dims, shards, least, high):
    def one(dim, blocks):
        heights = jax.random.uniform(jax.random.fold_in(jax.random.fold_in(own_key, 6), dim), (blocks,), jnp.float32, least / len(shards), high / len(shards))
        return jnp.repeat(jnp.exp(heights), dims[dim] // blocks).reshape((-1,) + (1,) * (len(dims) - dim - 1))

    factor_of = one(*shards[0])
    for cut in shards[1:]:
        factor_of = factor_of * one(*cut)
    return factor_of


def centred(key, shape, spread, reach, cuts=(), held_as=jnp.bfloat16):
    gain = block_scale(key, shape, cuts, -0.22, 0.18) if cuts else 1.0
    values = jax.random.normal(key, shape, jnp.float32) * spread * gain
    return jnp.minimum(jnp.maximum(values, -reach), reach).astype(held_as)


def setup_inputs(seed: int = 0) -> dict:
    splits = jax.random.split(jax.random.key(seed), 7)
    queries = centred(splits[0], (TOKENS, HEADS * HEAD_DIM), 1.0, 6.0, ((0, 32),))
    keys = draw_keys(jax.random.fold_in(splits[6], 71), 0)
    values = centred(splits[2], (TOKENS, HEADS * HEAD_DIM), 1.0, 6.0, ((0, 32),))
    forget = draw_forget(jax.random.fold_in(splits[6], 71), 0)
    beta = draw_beta(jax.random.fold_in(splits[6], 71), 0)
    level_weights = jnp.clip(jnp.exp(math.log(2.0) - 2.0794415 * jax.random.uniform(splits[5], (LEVELS + 1, TOKENS, HEADS), jnp.float32) ** block_scale(splits[5], (LEVELS + 1, TOKENS, HEADS), ((1, 32),), -0.2, 0.2)), 0.25, 2.0)
    return {"queries": queries, "keys": keys, "values": values, "forget": forget, "beta": beta, "level_weights": level_weights}


def contract(form, left, right):
    return jnp.einsum(form, left, right, precision=lax.Precision.HIGHEST)

def unit_rows(array):
    return array * lax.rsqrt(lax.optimization_barrier(jnp.sum(array * array, -1, keepdims=True)) + 1e-06)

def block_step(carry, pieces):
    memory, transition = carry
    query_block, key_block, value_block, forget_block, beta_block = pieces
    length = query_block.shape[0]
    head_dim = query_block.shape[-1]
    query_heads = unit_rows(jnp.swapaxes(query_block.astype(jnp.float32), 0, 1))
    key_heads = unit_rows(jnp.swapaxes(key_block.astype(jnp.float32), 0, 1))
    value_heads = jnp.swapaxes(value_block.astype(jnp.float32), 0, 1)
    decays = jnp.exp(-jnp.cumsum(forget_block, 0)).T
    strength = beta_block.T
    strict = jnp.tril(jnp.ones((length, length), jnp.float32), -1)
    causal = jnp.tril(jnp.ones((length, length), jnp.float32), 0)
    intersections = contract('hsk,htk->hst', key_heads, key_heads)
    unit_lower = jnp.eye(length, dtype=jnp.float32) + strength[:, :, None] * intersections * strict
    right_sides = jnp.concatenate([strength[:, :, None] * key_heads, (strength / decays)[:, :, None] * value_heads], -1)
    solved = lax.linalg.triangular_solve(unit_lower, right_sides, left_side=True, lower=True, unit_diagonal=True)
    update_rows = solved[..., :head_dim]
    write_rows = solved[..., head_dim:]
    scores = contract('htk,hsk->hts', query_heads, key_heads) * causal
    reached = decays[:, :, None] * (query_heads - contract('hts,hsk->htk', scores, update_rows))
    inside = decays[:, :, None] * contract('hts,hsv->htv', scores, write_rows) + contract('hvk,htk->htv', memory, reached)
    reach_dev = contract('hkj,htj->htk', transition, reached)
    final_decay = decays[:, -1][:, None, None]
    step_trans = final_decay * (jnp.eye(head_dim, dtype=jnp.float32) - contract('hsk,hsj->hkj', update_rows, key_heads))
    step_write = final_decay * contract('hsv,hsk->hvk', write_rows, key_heads)
    memory = contract('hvk,hkj->hvj', memory, step_trans) + step_write
    transition = contract('hik,hkj->hij', transition, step_trans)
    return ((memory, transition), (inside, reach_dev))

def reference(queries, keys, values, forget, beta, level_weights):
    devices = N_GRP * N_SEQ
    blocks = TOK_DEV // BLOCK

    def per_device(array):
        return array.reshape((devices, blocks, BLOCK) + array.shape[1:])
    shaped = (TOKENS, HEADS, HEAD_DIM)
    weights_dev = jnp.transpose(level_weights, (1, 0, 2)).reshape(devices, TOK_DEV, LEVELS + 1, HEADS)
    items = (per_device(queries.reshape(shaped)), per_device(keys.reshape(shaped)), per_device(values.reshape(shaped)), per_device(forget), per_device(beta), weights_dev, jnp.arange(devices, dtype=jnp.int32))
    spans = jnp.left_shift(jnp.int32(1), jnp.arange(LEVELS, dtype=jnp.int32))

    def device_step(levels, entry):
        query_dev, key_dev, value_dev, forget_dev, beta_dev, weight_dev, number = entry
        start = (jnp.zeros((HEADS, HEAD_DIM, HEAD_DIM), jnp.float32), jnp.broadcast_to(jnp.eye(HEAD_DIM, dtype=jnp.float32), (HEADS, HEAD_DIM, HEAD_DIM)))
        (memory, transition), (inside, reached) = lax.scan(block_step, start, (query_dev, key_dev, value_dev, forget_dev, beta_dev))
        inside = jnp.swapaxes(inside, 0, 1).reshape(HEADS, TOK_DEV, HEAD_DIM)
        reached = jnp.swapaxes(reached, 0, 1).reshape(HEADS, TOK_DEV, HEAD_DIM)
        weighted = jnp.transpose(weight_dev[:, 1:, :], (1, 2, 0))[:, :, :, None] * reached[None]
        far_part = contract('lhtk,lhvk->htv', weighted, levels)
        result = weight_dev[:, 0, :].T[:, :, None] * inside + far_part
        following = number + 1
        below = following % (2 * spans) == 0
        target = jnp.logical_and(following % spans == 0, jnp.logical_not(below))
        moved = contract('lhvk,hkj->lhvj', levels, transition)
        merged = contract('lhvk,hkj->hvj', levels * below.astype(jnp.float32)[:, None, None, None], transition) + memory
        cleared = jnp.logical_or(below, target)[:, None, None, None]
        levels = jnp.where(cleared, jnp.zeros_like(moved), moved) + target.astype(jnp.float32)[:, None, None, None] * merged[None]
        return (levels, result)
    zeros = jnp.zeros((LEVELS, HEADS, HEAD_DIM, HEAD_DIM), jnp.float32)
    unused, results = lax.scan(device_step, zeros, items)
    return jnp.transpose(results, (0, 2, 1, 3)).reshape(TOKENS, HEADS * HEAD_DIM)
```

```python
import functools

import jax
import jax.numpy as jnp
from jax import lax
from jax.experimental import pallas as pl
from jax.experimental.pallas import tpu as pltpu
from jax.sharding import PartitionSpec as P

MESH = pl.DeviceIdType.MESH
F32 = jnp.float32
BF16 = jnp.bfloat16
NN = (((1,), (0,)), ((), ()))
NT = (((1,), (1,)), ((), ()))
AUX = 16


def group_bits(heads, n_seq):
    need = heads.bit_length() - 1
    return tuple(range(need - 1)) + (n_seq.bit_length() - 1,)


def dot(a, b, dims=NN):
    return lax.dot_general(a, b, dims, preferred_element_type=F32)


def split(a):
    high = a.astype(BF16)
    return high, (a - high.astype(F32)).astype(BF16)


def mm(a, b, dims=NN):
    ah, al = a
    bh, bl = b
    return dot(ah, bh, dims) + (dot(ah, bl, dims) + dot(al, bh, dims))


def mm_exact(a, b):
    high, low = split(a)
    return dot(high, b) + dot(low, b)


def unit_lower_inverse(lowers, size, row, col):
    apart = row ^ col
    eye = (apart == 0).astype(F32)
    inverses = [eye - jnp.where(apart == 1, low, 0.0) for low in lowers]
    width = 2
    while width < size:
        mask = (apart >= width) & (apart < 2 * width)
        parts = [split(x) for x in inverses]
        blocks = [split(jnp.where(mask, low, 0.0)) for low in lowers]
        left = [split(mm(x, b)) for x, b in zip(parts, blocks)]
        inverses = [x - mm(l, p) for x, l, p in zip(inverses, left, parts)]
        width *= 2
    return inverses


def transitions(blocks, size, dim):
    row = lax.broadcasted_iota(jnp.int32, (size, size), 0)
    col = lax.broadcasted_iota(jnp.int32, (size, size), 1)
    staged = []
    lowers = []
    for block in blocks:
        k, v, aux = block[:size], block[size : 2 * size], block[2 * size :]
        cols = aux.T
        rk = lax.rsqrt(jnp.sum(k * k, -1, keepdims=True) + 1e-06)
        rk_row = jnp.broadcast_to(rk, (size, size)).T
        kb, vb = k.astype(BF16), v.astype(BF16)
        lowers.append(jnp.where(row > col, dot(kb, kb, NT) * rk * rk_row * cols[:, 1:2], 0.0))
        staged.append((kb, vb, rk, rk_row, aux[0:1], aux[1:2], cols))
    inverses = unit_lower_inverse(lowers, size, row, col)
    results = []
    eye = (row == col).astype(F32)
    for inverse, (kb, vb, rk, rk_row, decay_row, beta_row, cols) in zip(inverses, staged):
        update = mm_exact(inverse * (rk_row * beta_row), kb)
        write = mm_exact(inverse * (beta_row / decay_row), vb)
        pair = jnp.concatenate([update, write], 1)
        last = decay_row[:, size - 1 : size]
        moved = mm_exact((pair * rk).T, kb)
        node = jnp.concatenate([last * (eye - moved[:dim]), last * moved[dim:]], 0)
        results.append((node, pair, cols, rk_row))
    return results


def local_reads(q, kb, pair, cols, rk_row, dim):
    size = q.shape[0]
    row = lax.broadcasted_iota(jnp.int32, (size, size), 0)
    col = lax.broadcasted_iota(jnp.int32, (size, size), 1)
    rq = lax.rsqrt(jnp.sum(q * q, -1, keepdims=True) + 1e-06)
    scores = jnp.where(row >= col, dot(q.astype(BF16), kb, NT) * rq * rk_row, 0.0)
    seen = mm(split(scores), split(pair))
    decay_col = cols[:, 0:1]
    return decay_col * (q * rq - seen[:, :dim]), decay_col * seen[:, dim:] * cols[:, 2:3]


def join(lower, upper, dim):
    both = mm(split(lower), split(upper[:dim]))
    return jnp.concatenate([both[:dim], both[dim:] + upper[dim:]], 0)


def kernel(n_grp, n_seq, heads, *refs):
    q_ref, k_ref, v_ref, aux_ref, out_ref = refs[:5]
    kv_out, q_out, kv_in, q_in, pairs, cols, rks, reach, acc, joined = refs[5:15]
    bits = group_bits(heads, n_seq)
    low_levels = len(bits) - 1
    cross = bits[-1]
    total_bits = (n_grp * n_seq).bit_length() - 1
    middle = list(range(low_levels, cross))
    upward = list(range(cross + 1, total_bits))
    refs = refs[15:]
    trees, refs = refs[:low_levels], refs[low_levels:]
    n_mid, n_up = len(middle), len(upward)
    mid_out, mid_in = refs[:n_mid], refs[n_mid : 2 * n_mid]
    refs = refs[2 * n_mid :]
    up_out, up_in = refs[:n_up], refs[n_up : 2 * n_up]
    s_kv, r_kv, s_q, r_q, s_mid, r_mid, s_up, r_up, s_out, r_out = refs[2 * n_up :]
    size = q_ref.shape[0]
    dim = q_ref.shape[1] // heads
    half = heads // 2
    pos = lax.axis_index("grp") * n_seq + lax.axis_index("seq")

    def bit_of(number, l):
        return (number // (1 << l)) % 2

    me = sum(bit_of(pos, l) * (1 << m) for m, l in enumerate(bits))
    base = pos - sum(bit_of(pos, l) * (1 << l) for l in bits)
    side, place = me // half, me % half

    def where_is(number):
        return (number // n_seq, number % n_seq)

    def member(i):
        return where_is(base + sum(bit_of(i, m) * (1 << l) for m, l in enumerate(bits)))

    def partner(l):
        return where_is(pos + (1 - 2 * bit_of(pos, l)) * (1 << l))

    def slot(rank, sign):
        far, r = rank // half, rank % half
        spot = (place + half + sign * 2 * (r // 2)) % half
        if r % 2:
            spot = spot + 1 - 2 * (spot % 2)
        which = 1 - side if far else side
        return which * half + spot

    def columns(i):
        return pl.ds(pl.multiple_of(i * dim, dim), dim)

    barrier = pltpu.get_barrier_semaphore()
    for rank in range(1, heads):
        pl.semaphore_signal(
            barrier, inc=1, device_id=member(slot(rank, 1)), device_id_type=MESH
        )
    for l in middle + upward:
        pl.semaphore_signal(barrier, inc=1, device_id=partner(l), device_id_type=MESH)
    for i in range(heads):
        part = slice(i * dim, (i + 1) * dim)
        kv_out[i, :size] = k_ref[:, part].astype(F32)
        kv_out[i, size : 2 * size] = v_ref[:, part].astype(F32)
        kv_out[i, 2 * size :] = aux_ref[i]
        q_out[i] = q_ref[:, part].astype(F32)
    pl.semaphore_wait(barrier, heads - 1 + n_mid + n_up)

    def remote(source, target, send, receive, device):
        copy = pltpu.make_async_remote_copy(
            src_ref=source,
            dst_ref=target,
            send_sem=send,
            recv_sem=receive,
            device_id=device,
            device_id_type=MESH,
        )
        return copy

    pending = []
    kv_copies, q_copies = [], []
    for out, into, send, receive, copies in (
        (kv_out, kv_in, s_kv, r_kv, kv_copies),
        (q_out, q_in, s_q, r_q, q_copies),
    ):
        for rank in range(1, heads):
            i = slot(rank, 1)
            copy = remote(out.at[i], into.at[me], send.at[rank], receive.at[rank], member(i))
            copy.start()
            copies.append(copy)
    pending += kv_copies + q_copies
    kv_in[me] = kv_out[me]
    q_in[me] = q_out[me]

    mid_copies = [{} for l in middle]

    def send_mid(m, which):
        copy = remote(
            mid_out[m].at[which],
            mid_in[m].at[which],
            s_mid.at[m, which],
            r_mid.at[m, which],
            partner(middle[m]),
        )
        copy.start()
        pending.append(copy)
        return copy

    first_mid = []
    for far in range(2):
        which = 1 - side if far else side
        for first in range(0, half, 2):
            slots = []
            for rank in (far * half + first, far * half + first + 1):
                if rank:
                    kv_copies[rank - 1].wait_recv()
                slots.append(slot(rank, -1))
            done = transitions([kv_in[i] for i in slots], size, dim)
            for i, (node, pair, col, rk_row) in zip(slots, done):
                trees[0][i] = node
                pairs[i] = pair
                cols[i] = col
                rks[i] = rk_row[:8]
        for m in range(low_levels):
            count = half >> (m + 1)
            for j in range(count):
                lower = trees[m][which * 2 * count + 2 * j]
                upper = trees[m][which * 2 * count + 2 * j + 1]
                node = join(lower, upper, dim)
                if m + 1 < low_levels:
                    trees[m + 1][which * count + j] = node
                else:
                    mid_out[0][which] = node
        first_mid.append(send_mid(0, which))

    def read(j, lower, l, gate=None):
        seen = mm(split(reach[j]), lower, NT)
        far = cols[j, :, 3 + l : 4 + l] * seen[:, seen.shape[1] - dim :]
        acc[j] += far if gate is None else jnp.where(gate, far, 0.0)
        if seen.shape[1] > dim:
            new = seen[:, :dim]
            reach[j] = new if gate is None else jnp.where(gate, new, reach[j])

    for first in range(0, heads, 2):
        for rank in (first, first + 1):
            if rank:
                q_copies[rank - 1].wait_recv()
            i = slot(rank, -1)
            rk_row = jnp.broadcast_to(rks[i][:1], (size, size))
            near = local_reads(
                q_in[i], kv_in[i, :size, :].astype(BF16), pairs[i], cols[i], rk_row, dim
            )
            reach[i], acc[i] = near
    for m in range(low_levels):
        for key in range(0, heads, 2 << m):
            lower = split(trees[m][key >> m])
            for j in range(key + (1 << m), key + (2 << m)):
                read(j, lower, m)

    copies = first_mid
    for m, l in enumerate(middle):
        upper_side = bit_of(pos, l) == 1
        following = []
        for far in range(2):
            which = 1 - side if far else side
            copies[far].wait_recv()
            peer, mine = mid_in[m][which], mid_out[m][which]
            lower = jnp.where(upper_side, peer, mine)
            upper = jnp.where(upper_side, mine, peer)
            node = join(lower, upper, dim)
            if m + 1 < n_mid:
                mid_out[m + 1][which] = node
                following.append(send_mid(m + 1, which))
            else:
                joined[which] = node
        copies = following

    node = join(joined[0], joined[1], dim)

    def send_up(m):
        copy = remote(up_out[m], up_in[m], s_up.at[m], r_up.at[m], partner(upward[m]))
        copy.start()
        pending.append(copy)
        return copy

    up_out[0][...] = node[dim:] if n_up == 1 else node
    copy = send_up(0)
    for m, l in enumerate(middle):
        gate = bit_of(pos, l) == 1
        for which in range(2):
            lower = split(mid_in[m][which])
            for j in range(which * half, (which + 1) * half):
                read(j, lower, l, gate)
    lower = split(joined[0])
    for j in range(half, heads):
        read(j, lower, cross)
    for m, l in enumerate(upward):
        gate = bit_of(pos, l) == 1
        copy.wait_recv()
        peer = up_in[m][...]
        if m + 1 < n_up:
            mine = up_out[m][...]
            node = join(jnp.where(gate, peer, mine), jnp.where(gate, mine, peer), dim)
            up_out[m + 1][...] = node[dim:] if m + 2 == n_up else node
            copy = send_up(m + 1)
        lower = split(peer)
        for rank in range(heads - 1, -1, -1):
            if m + 1 < n_up:
                read(rank, lower, l, gate)
                continue
            i = slot(rank, 1)
            read(i, lower, l, gate)
            if rank == 0:
                out_ref[:, columns(me)] = acc[me]
                continue
            back = remote(
                acc.at[i], out_ref.at[:, columns(me)], s_out.at[rank], r_out.at[rank], member(i)
            )
            back.start()
            pending.append(back)
    for rank in range(1, heads):
        source = slot(rank, -1)
        remote(
            acc.at[source],
            out_ref.at[:, columns(source)],
            s_out.at[rank],
            r_out.at[rank],
            member(source),
        ).wait_recv()
    for copy in pending:
        copy.wait_send()


def on_device(n_grp, n_seq, queries, keys, values, forget, beta, level_weights):
    size = queries.shape[0]
    heads = forget.shape[1]
    dim = queries.shape[1] // heads
    levels = level_weights.shape[0]
    bits = group_bits(heads, n_seq)
    total_bits = (n_grp * n_seq).bit_length() - 1
    low_levels, cross = len(bits) - 1, bits[-1]
    n_mid, n_up = cross - low_levels, total_bits - cross - 1
    decays = jnp.exp(-jnp.cumsum(forget, 0)).T
    small = jnp.concatenate(
        [
            decays[:, None],
            beta.T[:, None],
            jnp.transpose(level_weights, (2, 0, 1)),
            jnp.zeros((heads, AUX - 2 - levels, size), F32),
        ],
        1,
    )
    mids = [pltpu.VMEM((2, 2 * dim, dim), F32)] * n_mid
    ups = [pltpu.VMEM((2 * dim, dim), F32)] * (n_up - 1) + [pltpu.VMEM((dim, dim), F32)]
    dma = pltpu.SemaphoreType.DMA
    return pl.pallas_call(
        functools.partial(kernel, n_grp, n_seq, heads),
        out_shape=jax.ShapeDtypeStruct((size, heads * dim), F32),
        in_specs=[pl.BlockSpec(memory_space=pltpu.VMEM)] * 4,
        out_specs=pl.BlockSpec(memory_space=pltpu.VMEM),
        scratch_shapes=[
            pltpu.VMEM((heads, 2 * size + AUX, dim), F32),
            pltpu.VMEM((heads, size, dim), F32),
            pltpu.VMEM((heads, 2 * size + AUX, dim), F32),
            pltpu.VMEM((heads, size, dim), F32),
            pltpu.VMEM((heads, size, 2 * dim), F32),
            pltpu.VMEM((heads, size, AUX), F32),
            pltpu.VMEM((heads, 8, size), F32),
            pltpu.VMEM((heads, size, dim), F32),
            pltpu.VMEM((heads, size, dim), F32),
            pltpu.VMEM((2, 2 * dim, dim), F32),
        ]
        + [pltpu.VMEM((heads >> m, 2 * dim, dim), F32) for m in range(low_levels)]
        + mids
        + mids
        + ups
        + ups
        + [dma((heads,))] * 4
        + [dma((n_mid, 2))] * 2
        + [dma((n_up,))] * 2
        + [dma((heads,))] * 2,
        compiler_params=pltpu.CompilerParams(collective_id=0, has_side_effects=True),
    )(queries, keys, values, small)


def solution(mesh):
    both = P(("grp", "seq"), None)
    return jax.shard_map(
        functools.partial(on_device, mesh.shape["grp"], mesh.shape["seq"]),
        mesh=mesh,
        in_specs=(both, both, both, both, both, P(None, ("grp", "seq"), None)),
        out_specs=both,
        check_vma=False,
    )
```

```python
import functools

import jax
import jax.numpy as jnp
from jax import lax
from jax.experimental import pallas as pl
from jax.experimental.pallas import tpu as pltpu
from jax.sharding import PartitionSpec as P

MESH = pl.DeviceIdType.MESH
F32 = jnp.float32
BF16 = jnp.bfloat16
NN = (((1,), (0,)), ((), ()))
NT = (((1,), (1,)), ((), ()))
AUX = 16


def group_bits(heads, n_seq):
    need = heads.bit_length() - 1
    return tuple(range(need - 1)) + (n_seq.bit_length() - 1,)


def dot(a, b, dims=NN):
    return lax.dot_general(a, b, dims, preferred_element_type=F32)


def split(a):
    high = a.astype(BF16)
    return high, (a - high.astype(F32)).astype(BF16)


def mm(a, b, dims=NN):
    ah, al = a
    bh, bl = b
    return dot(ah, bh, dims) + (dot(ah, bl, dims) + dot(al, bh, dims))


def mm_exact(a, b):
    high, low = split(a)
    return dot(high, b) + dot(low, b)


def unit_lower_inverse(lowers, size, row, col):
    apart = row ^ col
    eye = (apart == 0).astype(F32)
    inverses = [eye - jnp.where(apart == 1, low, 0.0) for low in lowers]
    width = 2
    while width < size:
        mask = (apart >= width) & (apart < 2 * width)
        parts = [split(x) for x in inverses]
        blocks = [split(jnp.where(mask, low, 0.0)) for low in lowers]
        left = [split(mm(x, b)) for x, b in zip(parts, blocks)]
        inverses = [x - mm(l, p) for x, l, p in zip(inverses, left, parts)]
        width *= 2
    return inverses


def transitions(blocks, size, dim):
    row = lax.broadcasted_iota(jnp.int32, (size, size), 0)
    col = lax.broadcasted_iota(jnp.int32, (size, size), 1)
    staged = []
    lowers = []
    for block in blocks:
        k, v, aux = block[:size], block[size : 2 * size], block[2 * size :]
        cols = aux.T
        rk = lax.rsqrt(jnp.sum(k * k, -1, keepdims=True) + 1e-06)
        rk_row = jnp.broadcast_to(rk, (size, size)).T
        kb, vb = k.astype(BF16), v.astype(BF16)
        lowers.append(jnp.where(row > col, dot(kb, kb, NT) * rk * rk_row * cols[:, 1:2], 0.0))
        staged.append((kb, vb, rk, rk_row, aux[0:1], aux[1:2], cols))
    inverses = unit_lower_inverse(lowers, size, row, col)
    results = []
    eye = (row == col).astype(F32)
    for inverse, (kb, vb, rk, rk_row, decay_row, beta_row, cols) in zip(inverses, staged):
        update = mm_exact(inverse * (rk_row * beta_row), kb)
        write = mm_exact(inverse * (beta_row / decay_row), vb)
        pair = jnp.concatenate([update, write], 1)
        last = decay_row[:, size - 1 : size]
        moved = mm_exact((pair * rk).T, kb)
        node = jnp.concatenate([last * (eye - moved[:dim]), last * moved[dim:]], 0)
        results.append((node, pair, cols, rk_row))
    return results


def local_reads(q, kb, pair, cols, rk_row, dim):
    size = q.shape[0]
    row = lax.broadcasted_iota(jnp.int32, (size, size), 0)
    col = lax.broadcasted_iota(jnp.int32, (size, size), 1)
    rq = lax.rsqrt(jnp.sum(q * q, -1, keepdims=True) + 1e-06)
    scores = jnp.where(row >= col, dot(q.astype(BF16), kb, NT) * rq * rk_row, 0.0)
    seen = mm(split(scores), split(pair))
    decay_col = cols[:, 0:1]
    return decay_col * (q * rq - seen[:, :dim]), decay_col * seen[:, dim:] * cols[:, 2:3]


def join(lower, upper, dim):
    both = mm(split(lower), split(upper[:dim]))
    return jnp.concatenate([both[:dim], both[dim:] + upper[dim:]], 0)


def kernel(n_grp, n_seq, heads, *refs):
    q_ref, k_ref, v_ref, aux_ref, out_ref = refs[:5]
    kv_out, q_out, kv_in, q_in, pairs, cols, rks, reach, acc, joined = refs[5:15]
    bits = group_bits(heads, n_seq)
    low_levels = len(bits) - 1
    cross = bits[-1]
    total_bits = (n_grp * n_seq).bit_length() - 1
    middle = list(range(low_levels, cross))
    upward = list(range(cross + 1, total_bits))
    refs = refs[15:]
    trees, refs = refs[:low_levels], refs[low_levels:]
    n_mid, n_up = len(middle), len(upward)
    mid_out, mid_in = refs[:n_mid], refs[n_mid : 2 * n_mid]
    refs = refs[2 * n_mid :]
    up_out, up_in = refs[:n_up], refs[n_up : 2 * n_up]
    s_kv, r_kv, s_q, r_q, s_mid, r_mid, s_up, r_up, s_out, r_out = refs[2 * n_up :]
    size = q_ref.shape[0]
    dim = q_ref.shape[1] // heads
    half = heads // 2
    pos = lax.axis_index("grp") * n_seq + lax.axis_index("seq")

    def bit_of(number, l):
        return (number // (1 << l)) % 2

    me = sum(bit_of(pos, l) * (1 << m) for m, l in enumerate(bits))
    base = pos - sum(bit_of(pos, l) * (1 << l) for l in bits)
    side, place = me // half, me % half

    def where_is(number):
        return (number // n_seq, number % n_seq)

    def member(i):
        return where_is(base + sum(bit_of(i, m) * (1 << l) for m, l in enumerate(bits)))

    def partner(l):
        return where_is(pos + (1 - 2 * bit_of(pos, l)) * (1 << l))

    def slot(rank, sign):
        far, r = rank // half, rank % half
        spot = (place + half + sign * 2 * (r // 2)) % half
        if r % 2:
            spot = spot + 1 - 2 * (spot % 2)
        which = 1 - side if far else side
        return which * half + spot

    def columns(i):
        return pl.ds(pl.multiple_of(i * dim, dim), dim)

    barrier = pltpu.get_barrier_semaphore()
    for rank in range(1, heads):
        pl.semaphore_signal(
            barrier, inc=1, device_id=member(slot(rank, 1)), device_id_type=MESH
        )
    for l in middle + upward:
        pl.semaphore_signal(barrier, inc=1, device_id=partner(l), device_id_type=MESH)
    for i in range(heads):
        part = slice(i * dim, (i + 1) * dim)
        kv_out[i, :size] = k_ref[:, part].astype(F32)
        kv_out[i, size : 2 * size] = v_ref[:, part].astype(F32)
        kv_out[i, 2 * size :] = aux_ref[i]
        q_out[i] = q_ref[:, part].astype(F32)
    pl.semaphore_wait(barrier, heads - 1 + n_mid + n_up)

    def remote(source, target, send, receive, device):
        copy = pltpu.make_async_remote_copy(
            src_ref=source,
            dst_ref=target,
            send_sem=send,
            recv_sem=receive,
            device_id=device,
            device_id_type=MESH,
        )
        return copy

    pending = []
    kv_copies, q_copies = {}, {}
    for out, into, send, receive, copies in (
        (kv_out, kv_in, s_kv, r_kv, kv_copies),
        (q_out, q_in, s_q, r_q, q_copies),
    ):
        for rank in range(1, heads):
            i = slot(rank, 1)
            copies[rank] = remote(
                out.at[i], into.at[me], send.at[rank], receive.at[rank], member(i)
            )
    for copy in kv_copies.values():
        copy.start()
    pending += list(kv_copies.values()) + list(q_copies.values())

    def send_queries(ranks):
        for rank in ranks:
            if 0 < rank < heads:
                q_copies[rank].start()

    send_queries((1, half, half + 1))
    kv_in[me] = kv_out[me]
    q_in[me] = q_out[me]

    mid_copies = [{} for l in middle]

    def send_mid(m, which):
        copy = remote(
            mid_out[m].at[which],
            mid_in[m].at[which],
            s_mid.at[m, which],
            r_mid.at[m, which],
            partner(middle[m]),
        )
        copy.start()
        pending.append(copy)
        return copy

    first_mid = []
    for far in range(2):
        which = 1 - side if far else side
        for first in range(0, half, 2):
            slots = []
            for rank in (far * half + first, far * half + first + 1):
                if rank:
                    kv_copies[rank].wait_recv()
                slots.append(slot(rank, -1))
            done = transitions([kv_in[i] for i in slots], size, dim)
            for i, (node, pair, col, rk_row) in zip(slots, done):
                trees[0][i] = node
                pairs[i] = pair
                cols[i] = col
                rks[i] = rk_row[:8]
        for m in range(low_levels):
            count = half >> (m + 1)
            for j in range(count):
                lower = trees[m][which * 2 * count + 2 * j]
                upper = trees[m][which * 2 * count + 2 * j + 1]
                node = join(lower, upper, dim)
                if m + 1 < low_levels:
                    trees[m + 1][which * count + j] = node
                else:
                    mid_out[0][which] = node
        first_mid.append(send_mid(0, which))
        send_queries(range(far * half + 2, far * half + half))

    def read(j, lower, l, gate=None):
        seen = mm(split(reach[j]), lower, NT)
        far = cols[j, :, 3 + l : 4 + l] * seen[:, seen.shape[1] - dim :]
        acc[j] += far if gate is None else jnp.where(gate, far, 0.0)
        if seen.shape[1] > dim:
            new = seen[:, :dim]
            reach[j] = new if gate is None else jnp.where(gate, new, reach[j])

    for first in range(0, heads, 2):
        for rank in (first, first + 1):
            if rank:
                q_copies[rank].wait_recv()
            i = slot(rank, -1)
            rk_row = jnp.broadcast_to(rks[i][:1], (size, size))
            near = local_reads(
                q_in[i], kv_in[i, :size, :].astype(BF16), pairs[i], cols[i], rk_row, dim
            )
            reach[i], acc[i] = near
    for m in range(low_levels):
        for key in range(0, heads, 2 << m):
            lower = split(trees[m][key >> m])
            for j in range(key + (1 << m), key + (2 << m)):
                read(j, lower, m)

    copies = first_mid
    for m, l in enumerate(middle):
        upper_side = bit_of(pos, l) == 1
        following = []
        for far in range(2):
            which = 1 - side if far else side
            copies[far].wait_recv()
            peer, mine = mid_in[m][which], mid_out[m][which]
            lower = jnp.where(upper_side, peer, mine)
            upper = jnp.where(upper_side, mine, peer)
            node = join(lower, upper, dim)
            if m + 1 < n_mid:
                mid_out[m + 1][which] = node
                following.append(send_mid(m + 1, which))
            else:
                joined[which] = node
        copies = following

    node = join(joined[0], joined[1], dim)

    def send_up(m):
        copy = remote(up_out[m], up_in[m], s_up.at[m], r_up.at[m], partner(upward[m]))
        copy.start()
        pending.append(copy)
        return copy

    up_out[0][...] = node[dim:] if n_up == 1 else node
    copy = send_up(0)
    for m, l in enumerate(middle):
        gate = bit_of(pos, l) == 1
        for which in range(2):
            lower = split(mid_in[m][which])
            for j in range(which * half, (which + 1) * half):
                read(j, lower, l, gate)
    lower = split(joined[0])
    for j in range(half, heads):
        read(j, lower, cross)
    for m, l in enumerate(upward):
        gate = bit_of(pos, l) == 1
        copy.wait_recv()
        peer = up_in[m][...]
        if m + 1 < n_up:
            mine = up_out[m][...]
            node = join(jnp.where(gate, peer, mine), jnp.where(gate, mine, peer), dim)
            up_out[m + 1][...] = node[dim:] if m + 2 == n_up else node
            copy = send_up(m + 1)
        lower = split(peer)
        for rank in range(heads - 1, -1, -1):
            if m + 1 < n_up:
                read(rank, lower, l, gate)
                continue
            i = slot(rank, 1)
            read(i, lower, l, gate)
            if rank == 0:
                out_ref[:, columns(me)] = acc[me]
                continue
            back = remote(
                acc.at[i], out_ref.at[:, columns(me)], s_out.at[rank], r_out.at[rank], member(i)
            )
            back.start()
            pending.append(back)
    for rank in range(1, heads):
        source = slot(rank, -1)
        remote(
            acc.at[source],
            out_ref.at[:, columns(source)],
            s_out.at[rank],
            r_out.at[rank],
            member(source),
        ).wait_recv()
    for copy in pending:
        copy.wait_send()


def on_device(n_grp, n_seq, queries, keys, values, forget, beta, level_weights):
    size = queries.shape[0]
    heads = forget.shape[1]
    dim = queries.shape[1] // heads
    levels = level_weights.shape[0]
    bits = group_bits(heads, n_seq)
    total_bits = (n_grp * n_seq).bit_length() - 1
    low_levels, cross = len(bits) - 1, bits[-1]
    n_mid, n_up = cross - low_levels, total_bits - cross - 1
    decays = jnp.exp(-jnp.cumsum(forget, 0)).T
    small = jnp.concatenate(
        [
            decays[:, None],
            beta.T[:, None],
            jnp.transpose(level_weights, (2, 0, 1)),
            jnp.zeros((heads, AUX - 2 - levels, size), F32),
        ],
        1,
    )
    mids = [pltpu.VMEM((2, 2 * dim, dim), F32)] * n_mid
    ups = [pltpu.VMEM((2 * dim, dim), F32)] * (n_up - 1) + [pltpu.VMEM((dim, dim), F32)]
    dma = pltpu.SemaphoreType.DMA
    return pl.pallas_call(
        functools.partial(kernel, n_grp, n_seq, heads),
        out_shape=pltpu.VMEM((size, heads * dim), F32),
        in_specs=[pl.BlockSpec(memory_space=pltpu.VMEM)] * 4,
        out_specs=pl.BlockSpec(memory_space=pltpu.VMEM),
        scratch_shapes=[
            pltpu.VMEM((heads, 2 * size + AUX, dim), F32),
            pltpu.VMEM((heads, size, dim), F32),
            pltpu.VMEM((heads, 2 * size + AUX, dim), F32),
            pltpu.VMEM((heads, size, dim), F32),
            pltpu.VMEM((heads, size, 2 * dim), F32),
            pltpu.VMEM((heads, size, AUX), F32),
            pltpu.VMEM((heads, 8, size), F32),
            pltpu.VMEM((heads, size, dim), F32),
            pltpu.VMEM((heads, size, dim), F32),
            pltpu.VMEM((2, 2 * dim, dim), F32),
        ]
        + [pltpu.VMEM((heads >> m, 2 * dim, dim), F32) for m in range(low_levels)]
        + mids
        + mids
        + ups
        + ups
        + [dma((heads,))] * 4
        + [dma((n_mid, 2))] * 2
        + [dma((n_up,))] * 2
        + [dma((heads,))] * 2,
        compiler_params=pltpu.CompilerParams(collective_id=0, has_side_effects=True),
    )(queries, keys, values, small)


def solution(mesh):
    both = P(("grp", "seq"), None)
    return jax.shard_map(
        functools.partial(on_device, mesh.shape["grp"], mesh.shape["seq"]),
        mesh=mesh,
        in_specs=(both, both, both, both, both, P(None, ("grp", "seq"), None)),
        out_specs=both,
        check_vma=False,
    )
```
